32 devices in a mesh: row: 4 (over z), col: 8 (over y, x, core).
Axes of the slice: x: 2, y: 2, z: 4, core: 2. Of those that a mesh axis runs over, the one named last changes fastest.
Arguments:
- a_matrix: float32 [16384, 16384], P('row', 'col'), may hold values from -2.25 to 2.25
- b_matrix: float32 [16384, 16384], P('row', 'col'), may hold values from -0.1 to 3.1
- x_block: float32 [16384, 64], P('row'), may hold values from -6 to 6
- r_block: float32 [16384, 64], P('row'), may hold values from -6 to 6
- p_block: float32 [16384, 64], P('row'), may hold values from -6 to 6
Outputs:
- x_next: float32 [16384, 64], P('row')
- r_next: float32 [16384, 64], P('row')
- p_next: float32 [16384, 64], P('row')
The draws below stay inside these ranges and needn't reach their ends.
All inputs are finite; a program needn't handle non-finite values.
Results may differ from the reference program's by a relative error of at most 0.0003.
Values sent between devices are 32-bit elements; how exact they have to be, the bound alone decides.
A program may use at most 192 MiB of HBM per device.

```python
import math
import jax
import jax.numpy as jnp
from jax import lax

N = 16384
K = 64
ITERS = 2
NS_STEPS = 8


def symmetric_field(key, spread, low, high):
    keys = jax.random.split(key, 2)
    noise = jax.random.normal(keys[0], (N, N), jnp.float32)
    mixed = (noise + noise.T) * (spread / math.sqrt(2.0 * N))
    diag_vals = jax.random.uniform(keys[1], (N,), jnp.float32, low, high)
    return mixed + jnp.diag(diag_vals)


def draw_a_matrix(key, part):
    return symmetric_field(jax.random.fold_in(key, 11), 0.5, -2.0, 2.0)


def draw_b_matrix(key, part):
    return symmetric_field(jax.random.fold_in(key, 23), 0.3, 1.5, 3.0)


def shard_levels(rng, shape, cuts, low, largest):
    level = 1.0
    for position, shards_of in cuts:
        heights = jax.random.uniform(jax.random.fold_in(jax.random.fold_in(rng, 6), position), (shards_of,), jnp.float32, low / len(cuts), largest / len(cuts))
        level = level * jnp.repeat(jnp.exp(heights), shape[position] // shards_of).reshape((-1,) + (1,) * (len(shape) - 1 - position))
    return level


def normal_values(own_key, shape, scale, most, cuts=(), held_as=jnp.bfloat16):
    entries = scale * jax.random.normal(own_key, shape, jnp.float32)
    if cuts:
        entries = entries * shard_levels(own_key, shape, cuts, -0.22, 0.18)
    return jnp.clip(entries, -most, most).astype(held_as)


def setup_inputs(seed: int = 0) -> dict:
    seeds = jax.random.split(jax.random.key(seed), 6)
    return {
        "a_matrix": draw_a_matrix(jax.random.fold_in(seeds[5], 71), 0),
        "b_matrix": draw_b_matrix(jax.random.fold_in(seeds[5], 71), 0),
        "x_block": normal_values(seeds[2], (N, K), 1.0, 6.0, ((0, 4),), jnp.float32),
        "r_block": normal_values(seeds[3], (N, K), 1.0, 6.0, ((0, 4),), jnp.float32),
        "p_block": normal_values(seeds[4], (N, K), 1.0, 6.0, ((0, 4),), jnp.float32),
    }


def matmul(left, right):
    return jnp.dot(left.astype(jnp.float32), right.astype(jnp.float32), precision=lax.Precision.HIGHEST, preferred_element_type=jnp.float32)

def ritz_step(gram_a, gram_b, count):
    gram_a = 0.5 * (gram_a + gram_a.T)
    gram_b = 0.5 * (gram_b + gram_b.T)
    lower = jnp.linalg.cholesky(gram_b)
    half = lax.linalg.triangular_solve(lower, gram_a, left_side=True, lower=True)
    middle = lax.linalg.triangular_solve(lower, half.T, left_side=True, lower=True)
    middle = 0.5 * (middle + middle.T)
    extent = middle.shape[0]
    ident = jnp.eye(extent, dtype=middle.dtype)
    shift = jnp.trace(middle) / extent
    centred = middle - shift * ident
    sign_est = centred / jnp.sqrt(jnp.sum(centred * centred) + 1e-06)
    for turn in range(NS_STEPS):
        sign_est = 1.5 * sign_est - 0.5 * matmul(sign_est, matmul(sign_est, sign_est))
    filtered = (0.5 * (ident - sign_est))[:, :count]
    coords = lax.linalg.triangular_solve(lower, filtered, left_side=True, lower=True, transpose_a=True) * math.sqrt(N)
    reduced = matmul(filtered.T, matmul(middle, filtered))
    return (coords, reduced)

def reference(a_matrix, b_matrix, x_block, r_block, p_block):
    for turn in range(ITERS):
        panel = jnp.concatenate([x_block, r_block, p_block], axis=1)
        prod_a = matmul(a_matrix, panel)
        prod_b = matmul(b_matrix, panel)
        coords, reduced = ritz_step(matmul(panel.T, prod_a), matmul(panel.T, prod_b), K)
        x_block = matmul(panel, coords)
        p_block = matmul(panel[:, K:], coords[K:])
        r_block = matmul(prod_a, coords) - matmul(matmul(prod_b, coords), reduced)
    return (x_block, r_block, p_block)
```

```python
import functools
import math

import jax
import jax.numpy as jnp
from jax import lax
from jax.experimental import pallas as pl
from jax.experimental.pallas import tpu as pltpu
from jax.sharding import PartitionSpec as P

NS_STEPS = 8
HIGHEST = lax.Precision.HIGHEST
HIGH = lax.Precision.HIGH


def mm(left, right, lc=1, rc=0, precision=HIGHEST):
    return lax.dot_general(
        left, right, (((lc,), (rc,)), ((), ())), precision=precision, preferred_element_type=jnp.float32
    )


def total(value):
    return lax.psum(lax.psum(value, "row"), "col")


def spread_t(value_t, tile_cols):
    ratio = lax.axis_size("col") // lax.axis_size("row")
    col_index = lax.axis_index("col")
    part = lax.dynamic_slice_in_dim(value_t, col_index % ratio * tile_cols, tile_cols, 1)
    kept = jnp.where(lax.axis_index("row") == col_index // ratio, part, 0.0)
    return lax.psum(kept, "row")


def block_inverse(block):
    size = block.shape[0]
    rows = lax.broadcasted_iota(jnp.int32, (size, size), 0)
    cols = lax.broadcasted_iota(jnp.int32, (size, size), 1)
    inverse = jnp.where(rows == cols, 1.0, 0.0)
    for j in range(size):
        pivot = 1.0 / block[j : j + 1, j : j + 1]
        factor = jnp.where(rows[:, :1] > j, block[:, j : j + 1], 0.0)
        inverse = inverse - factor * (inverse[j : j + 1] * pivot)
        block = block - factor * (block[j : j + 1] * pivot)
    diag = jnp.sum(jnp.where(rows == cols, block, 0.0), axis=1, keepdims=True)
    return inverse / jnp.sqrt(diag)


def ritz_kernel(order, ga_ref, gb_ref, w_ref, ch_ref, wa_ref, wb_ref, linv_ref, sym_ref):
    n, k = w_ref.shape[0], ch_ref.shape[1]
    gb = gb_ref[...]
    sym_ref[...] = 0.5 * (gb + gb.T)
    ga = ga_ref[...]
    ga = 0.5 * (ga + ga.T)
    nb = n // k
    cut = lambda ref, i, j: ref[i * k : (i + 1) * k, j * k : (j + 1) * k]
    linv_ref[...] = jnp.zeros((n, n), jnp.float32)
    low, inv = {}, {}
    for j in range(nb):
        for i in range(j, nb):
            rest = cut(sym_ref, i, j)
            for m in range(j):
                rest = rest - mm(low[i, m], low[j, m], 1, 1)
            if i == j:
                inv[j, j] = block_inverse(rest)
            else:
                low[i, j] = mm(rest, inv[j, j], 1, 1)
    for j in range(nb):
        for i in range(j + 1, nb):
            total = mm(low[i, j], inv[j, j])
            for m in range(j + 1, i):
                total = total + mm(low[i, m], inv[m, j])
            inv[i, j] = -mm(inv[i, i], total)
    for (i, j), value in inv.items():
        linv_ref[i * k : (i + 1) * k, j * k : (j + 1) * k] = value
    linv = linv_ref[...]
    linv_t = linv.T
    middle = mm(mm(linv, ga), linv_t)
    middle = 0.5 * (middle + middle.T)
    rows = lax.broadcasted_iota(jnp.int32, (n, n), 0)
    cols = lax.broadcasted_iota(jnp.int32, (n, n), 1)
    ident = jnp.where(rows == cols, 1.0, 0.0)
    shift = jnp.sum(middle * ident) / n
    centred = middle - shift * ident
    sign_est = centred / jnp.sqrt(jnp.full((1, 1), jnp.sum(centred * centred) + 1e-06))
    for turn in range(NS_STEPS):
        sign_est = 1.5 * sign_est - 0.5 * mm(sign_est, mm(sign_est, sign_est))
    filtered = (0.5 * (ident - sign_est))[:, :k]
    coords = mm(linv_t, filtered) * math.sqrt(order)
    reduced = mm(filtered.T, mm(middle, filtered))
    ch_ref[...] = mm(coords, reduced)
    w_ref[:, :k] = coords
    w_ref[:, k:] = jnp.where(lax.broadcasted_iota(jnp.int32, (n, k), 0) >= k, coords, 0.0)
    w = w_ref[...]
    w_t = w.T
    wa_ref[...] = mm(w_t, mm(ga, w))
    wb_ref[...] = mm(w_t, mm(sym_ref[...], w))


def ritz(order, width, gram_a, gram_b):
    n, k = gram_a.shape[0], width
    shape = lambda *dims: jax.ShapeDtypeStruct(dims, jnp.float32)
    return pl.pallas_call(
        functools.partial(ritz_kernel, order),
        out_shape=(shape(n, 2 * k), shape(n, k), shape(2 * k, 2 * k), shape(2 * k, 2 * k)),
        in_specs=[pl.BlockSpec(memory_space=pltpu.VMEM)] * 2,
        out_specs=[pl.BlockSpec(memory_space=pltpu.VMEM)] * 4,
        scratch_shapes=[pltpu.VMEM((n, n), jnp.float32)] * 2,
        name="ritz",
    )(gram_a, gram_b)


def extend(kept, fresh):
    k = fresh.shape[1]
    x, r, p = fresh[:k], fresh[k : 2 * k], fresh[2 * k :]
    return jnp.concatenate(
        [
            jnp.concatenate([kept[:k, :k], x, kept[:k, k:]], axis=1),
            jnp.concatenate([x.T, r, p.T], axis=1),
            jnp.concatenate([kept[k:, :k], p, kept[k:, k:]], axis=1),
        ],
        axis=0,
    )


def local(order, a_matrix, b_matrix, x_block, r_block, p_block):
    tile_cols = a_matrix.shape[1]
    k = x_block.shape[1]
    panel = jnp.concatenate([x_block, r_block, p_block], axis=1)
    matched_t = spread_t(panel.T, tile_cols)
    prod_a = mm(a_matrix, matched_t, 1, 1, HIGH)
    prod_b = mm(b_matrix, matched_t, 1, 1, HIGH)
    grams = total(jnp.concatenate([mm(panel, prod_a, 0, 0), mm(panel, prod_b, 0, 0)], axis=1))
    w, ch, kept_a, kept_b = ritz(order, k, grams[:, : 3 * k], grams[:, 3 * k :])
    coords = w[:, :k]
    resid_t = lax.psum(mm(coords, prod_a, 0, 1) - mm(ch, prod_b, 0, 1), "col")
    matched_t = spread_t(resid_t, tile_cols)
    both = mm(panel, w)
    panel = jnp.concatenate([both[:, :k], resid_t.T, both[:, k:]], axis=1)
    fresh_a = mm(a_matrix, matched_t, 1, 1, HIGH)
    fresh_b = mm(b_matrix, matched_t, 1, 1, HIGH)
    grams = total(jnp.concatenate([mm(panel, fresh_a, 0, 0), mm(panel, fresh_b, 0, 0)], axis=1))
    w2, ch2, _, _ = ritz(order, k, extend(kept_a, grams[:, :k]), extend(kept_b, grams[:, k:]))
    c2 = w2[:, :k]
    outer = lambda c: jnp.concatenate([c[:k], c[2 * k :]], axis=0)
    on_a, on_b = mm(w, outer(c2)), mm(w, outer(ch2))
    resid_t = lax.psum(
        (mm(on_a, prod_a, 0, 1) + mm(c2[k : 2 * k], fresh_a, 0, 1))
        - (mm(on_b, prod_b, 0, 1) + mm(ch2[k : 2 * k], fresh_b, 0, 1)),
        "col",
    )
    both = mm(panel, w2)
    return (both[:, :k], resid_t.T, both[:, k:])


def solution(mesh):
    def whole(a_matrix, b_matrix, x_block, r_block, p_block):
        return jax.shard_map(
            functools.partial(local, a_matrix.shape[0]),
            mesh=mesh,
            in_specs=(P("row", "col"), P("row", "col"), P("row", None), P("row", None), P("row", None)),
            out_specs=(P("row", None), P("row", None), P("row", None)),
            check_vma=False,
        )(a_matrix, b_matrix, x_block, r_block, p_block)

    return whole
```
